512 devices in a mesh: group: 16 (over z), dev: 32 (over y, x, core).
Axes of the slice: x: 4, y: 4, z: 16, core: 2. Of those that a mesh axis runs over, the one named last changes fastest.
Arguments:
- embeddings: float32 [1024, 128, 512], P(('group', 'dev')), may hold values from -6 to 6
- neighbours: int32 [1024, 8], P(('group', 'dev')), may hold values from 0 to 1023, as said below
Outputs:
- diffused: float32 [1024, 128, 512], P(('group', 'dev'))
The draws below stay inside these ranges and needn't reach their ends.
Inputs may be any that keep to these rules, and one draw needn't show every extreme that they name: `neighbours`: blocks are numbered device after device in the mesh order, 2 to a device. For a block on device (g, d): entries 0 to 3 name other blocks of the same device; entries 4 to 6 name blocks of group g on devices other than d, and the blocks of one device name at most 1 block of any one other device this way, a bound that some device of every group receives from each other device of the group; the last entry names a block of group (g + 1) mod the number of groups on dev index d.
All inputs are finite; a program needn't handle non-finite values.
Results may differ from the reference program's by a relative error of at most 0.0014.
Values may be sent and summed in bfloat16 or wider, within the bound.
No kernel may reach another device: no remote copies, remote signals or barrier semaphores. Data moves between devices by JAX's collectives and lax.ppermute only.
A program may use at most 128 MiB of HBM per device.

```python
import jax
import jax.numpy as jnp
from jax import lax

E = 512
R = 128
KO = 4
KI = 3
BPD = 2
CAP = 1
NB = 1024
N_GROUP = 16
N_DEV = 32


def shuffled(subkey):
    return jax.random.permutation(subkey, N_DEV - 2).astype(jnp.int32)


def draw_neighbours(key, part):
    subkeys = jax.random.split(key, 5)
    devices = N_GROUP * N_DEV
    requests = BPD * KI
    device_ids = jnp.arange(devices, dtype=jnp.int32)
    group_of = device_ids // N_DEV
    place_of = device_ids % N_DEV
    block_ids = jnp.arange(BPD * devices, dtype=jnp.int32)
    home_block = block_ids // BPD * BPD
    own_slot = block_ids % BPD
    shifted = jax.random.randint(subkeys[0], (BPD * devices, KO), 1, BPD)
    local_part = home_block[:, None] + (own_slot[:, None] + shifted) % BPD
    busiest = jax.random.randint(subkeys[1], (N_GROUP,), 0, N_DEV)
    toward = (busiest[group_of] - place_of) % N_DEV
    toward = jnp.where(toward == 0, 1, toward)
    orders = jax.vmap(shuffled)(jax.random.split(subkeys[2], devices))
    bucket = jnp.arange(requests, dtype=jnp.int32) // CAP
    picked = orders[:, jnp.maximum(bucket - 1, 0)]
    offset = jnp.where(bucket[None, :] == 0, toward[:, None], 1 + (toward[:, None] + picked) % (N_DEV - 1))
    target_dev = (place_of[:, None] + offset) % N_DEV
    target_slot = jax.random.randint(subkeys[3], (devices, requests), 0, BPD)
    inner_part = ((group_of[:, None] * N_DEV + target_dev) * BPD + target_slot).reshape(BPD * devices, KI)
    upper_group = (group_of + 1) % N_GROUP
    cross_slot = jax.random.randint(subkeys[4], (BPD * devices,), 0, BPD)
    cross_part = (jnp.repeat(upper_group * N_DEV + place_of, BPD) * BPD + cross_slot)[:, None]
    return jnp.concatenate([local_part, inner_part, cross_part], axis=1).astype(jnp.int32)


def steps_of(key, dims, cuts, low, largest):
    def one(axis_at, parts):
        steps = jax.random.uniform(jax.random.fold_in(jax.random.fold_in(key, 6), axis_at), (parts,), jnp.float32, low / len(cuts), largest / len(cuts))
        return jnp.repeat(jnp.exp(steps), dims[axis_at] // parts).reshape((-1,) + (1,) * (len(dims) - axis_at - 1))

    gain = one(*cuts[0])
    for cut in cuts[1:]:
        gain = gain * one(*cut)
    return gain


def scatter_about(rng, extent, width, most, cuts=(), kind=jnp.bfloat16):
    gain = steps_of(rng, extent, cuts, -0.22, 0.18) if cuts else 1.0
    values = jax.random.normal(rng, extent, jnp.float32) * width * gain
    return jnp.minimum(jnp.maximum(values, -most), most).astype(kind)


def setup_inputs(seed: int = 0) -> dict:
    key_of = jax.random.split(jax.random.key(seed), 3)
    embeddings = scatter_about(key_of[0], (NB, R, E), 1.0, 6.0, ((0, 512),), jnp.float32)
    neighbours = draw_neighbours(jax.random.fold_in(key_of[2], 71), 0)
    return {"embeddings": embeddings, "neighbours": neighbours}


inv_band = 40.0
eps = 1e-06

def reference(embeddings, neighbours):
    rounded = embeddings.astype(jnp.bfloat16)
    widened = rounded.astype(jnp.float32)
    scales = lax.rsqrt(lax.optimization_barrier(jnp.mean(widened * widened, axis=-1)) + eps)
    features = embeddings.shape[-1]
    highest = lax.Precision.HIGHEST

    def visit_block(state_pair, block_at):
        pulled, degree = state_pair
        listed = neighbours[block_at]
        own_rows = widened[block_at]
        far_rows = widened[listed]
        inner_prod = jnp.einsum('re,kqe->krq', own_rows, far_rows, precision=highest)
        kernel = jnp.exp(inv_band * inner_prod * scales[block_at][None, :, None] * scales[listed][:, None, :] / features)
        weights = lax.optimization_barrier(kernel.astype(jnp.bfloat16)).astype(jnp.float32)
        forward = jnp.einsum('krq,kqe->re', weights, far_rows, precision=highest)
        backward = jnp.einsum('krq,re->kqe', weights, own_rows, precision=highest)
        pulled = pulled.at[block_at].add(forward).at[listed].add(backward)
        degree = degree.at[block_at].add(lax.optimization_barrier(jnp.sum(kernel, axis=(0, 2)))).at[listed].add(lax.optimization_barrier(jnp.sum(kernel, axis=1)))
        return ((pulled, degree), None)
    initial = (jnp.zeros(embeddings.shape, jnp.float32), jnp.zeros(embeddings.shape[:2], jnp.float32))
    outcome = lax.scan(visit_block, initial, jnp.arange(embeddings.shape[0], dtype=jnp.int32))
    pulled, degree = outcome[0]
    return 0.5 * embeddings + 0.5 * pulled / degree[:, :, None]
```

```python
import jax
import jax.numpy as jnp
from jax import lax
from jax.experimental import pallas as pl
from jax.experimental.pallas import tpu as pltpu
from jax.sharding import PartitionSpec as P

KO = 4
KI = 3
R = 128
E = 512
SIDE = 4
ROWS = 2 * R + 8
ORDER = (3, 1, 2)
TOGETHER = 4

inv_band = 40.0
eps = 1e-06

f32 = jnp.float32
bf16 = jnp.bfloat16


def whole():
    return pl.BlockSpec(memory_space=pltpu.VMEM)


def scalars():
    return pl.BlockSpec(memory_space=pltpu.SMEM)


def call(kernel, out_shape, in_specs, flops, nbytes, scratch=()):
    return pl.pallas_call(
        kernel,
        out_shape=out_shape,
        in_specs=in_specs,
        scratch_shapes=scratch,
        out_specs=jax.tree.map(lambda _: whole(), out_shape),
        cost_estimate=pl.CostEstimate(flops=flops, bytes_accessed=nbytes, transcendentals=0),
        compiler_params=pltpu.CompilerParams(vmem_limit_bytes=16 << 20),
    )


def array(shape, dtype):
    return jax.ShapeDtypeStruct(shape, dtype)


def pack_kernel(lists, rows, packed, names_at, rows_at, sems):
    copies = [
        pltpu.make_async_copy(rows.at[n // 2, at], rows_at.at[n // 2, at], sems.at[n])
        for n in range(4)
        for at in (pl.ds(n % 2 * (R // 2), R // 2),)
    ]
    listing = pltpu.make_async_copy(lists, names_at, sems.at[4])
    listing.start()
    for copy in copies:
        copy.start()
    listing.wait()
    at = lax.broadcasted_iota(jnp.int32, (8, E), 0)
    names = jnp.zeros((8, E), jnp.int32)
    for b in range(2):
        for j in range(KI + 1):
            name = names_at[b, KO + j]
            name = name % 64 if j < KI else name % 2
            names = jnp.where(at == 4 * b + j, name, names)
    packed[2 * R :, :] = names.astype(f32).astype(bf16)
    for n, copy in enumerate(copies):
        copy.wait()
        half = n % 2 * (R // 2)
        packed[n * (R // 2) : (n + 1) * (R // 2), :] = rows_at[n // 2, half : half + R // 2].astype(bf16)


def column_scale(q):
    wide = q.astype(f32)
    return lax.rsqrt(jnp.sum(wide * wide, axis=1, keepdims=True) * (1.0 / E) + eps)


def tiles(jobs, turned, scale, sums):
    weighted = []
    for q, p, times in jobs:
        inner = jnp.dot(q, turned[p], preferred_element_type=f32)
        kernel = jnp.exp(inner * column_scale(q) * scale[p, 0:1, :])
        weighted.append(kernel * times)
    pulled = [
        lax.dot_general(
            w.astype(bf16), q, (((0,), (0,)), ((), ())), preferred_element_type=f32
        )
        for (q, p, times), w in zip(jobs, weighted)
    ]
    for (q, p, times), w, rows in zip(jobs, weighted, pulled):
        sums[p, R : R + 1, :R] += jnp.sum(w, axis=0, keepdims=True)
        sums[p, :R, :] += rows


def local_kernel(own, other, turned, scale, asked, sums):
    lane = lax.broadcasted_iota(jnp.int32, (1, E), 1) // R
    for n, (rows, b) in enumerate(((own, 0), (own, 1), (other, 0), (other, 1))):
        block = rows[b * R : (b + 1) * R, :]
        turned[n] = block.T
        column = column_scale(block) * (inv_band / E)
        scale[n] = jnp.broadcast_to(column, (R, R)).T[:8]
    own_names = own[2 * R :, :].astype(f32)
    other_names = other[2 * R :, :].astype(f32)
    for j in range(KI):
        asked[j : j + 1, :] = jnp.where(
            lane < 2,
            jnp.where(lane == 0, own_names[j : j + 1], own_names[4 + j : 5 + j]),
            jnp.where(lane == 2, other_names[j : j + 1], other_names[4 + j : 5 + j]),
        )
    sums[...] = jnp.zeros(sums.shape, f32)
    tiles(
        [(own[(1 - b) * R : (2 - b) * R, :], b, 2.0 * KO) for b in range(2)],
        turned,
        scale,
        sums,
    )


def across_kernel(place, own, other, across, turned, scale, sums_in, sums):
    sums[...] = sums_in[...]
    upper = place[1] == 1
    jobs = []
    for n, rows in enumerate((own, other)):
        near_names = rows[2 * R :, :].astype(f32)
        far_names = across[n, 2 * R :, :].astype(f32)
        for b in range(2):
            row = 4 * b + KI
            ours = jnp.max(near_names[row : row + 1, :R]).astype(jnp.int32)
            named = jnp.max(far_names[row : row + 1, :R]).astype(jnp.int32)
            far = jnp.clip(jnp.where(upper, ours, b), 0, 1)
            near = jnp.clip(jnp.where(upper, b, named), 0, 1)
            q = across[n, pl.ds(pl.multiple_of(far * R, R), R), :]
            jobs.append((q, 2 * n + near, 1.0))
    tiles(jobs, turned, scale, sums)


def partner(at, swap):
    near = at + 1 - 2 * (at % 2)
    away = SIDE - 1 - at
    return jnp.where(swap == 0, at, jnp.where(swap == 1, near, jnp.where(swap == 2, away, (at + 2) % SIDE)))


def pairs_of(far, second, place, asked, jobs):
    dev = place[0]
    y, x, core = dev // 8, dev // 2 % SIDE, dev % 2
    lane = lax.broadcasted_iota(jnp.int32, (1, E), 1) // R
    code = jnp.where(lane < 2, dev * 2 + lane, (dev + 1 - 2 * core) * 2 + lane - 2).astype(f32)
    digits = jnp.zeros((1, E), f32)
    for k, first in enumerate((0,) + ORDER):
        from_x = partner(x, jnp.where(core == 0, first, second))
        from_y = partner(y, jnp.where(core == 0, second, first))
        source = (from_y * SIDE + from_x) * 2 + core
        names = far[k, 2 * R :, :].astype(f32)
        for b in range(2):
            block = (source * 2 + b).astype(f32)
            count = jnp.zeros((1, E), f32)
            for j in range(KI):
                count += jnp.where(names[4 * b + j : 4 * b + j + 1] == code, 1.0, 0.0)
                count += jnp.where(asked[j : j + 1, :] == block, 1.0, 0.0)
            digits += count * float(4 ** (2 * k + b))
    total = jnp.int32(0)
    for p in range(4):
        word = jnp.max(digits[:, p * R : (p + 1) * R]).astype(jnp.int32)
        for n in range(2 * SIDE):
            times = (word >> (2 * n)) & 3
            jobs[0, total] = n
            jobs[1, total] = p
            jobs[2, total] = times
            total = total + jnp.where(times > 0, 1, 0)
    for n in range(TOGETHER - 1):
        jobs[0, total + n] = 0
        jobs[1, total + n] = 0
        jobs[2, total + n] = 0
    return total


def add_far(far, second, place, turned, scale, asked, sums, jobs):
    total = pairs_of(far, second, place, asked, jobs)

    def some(i, carry):
        taken = []
        for t in range(TOGETHER):
            n, p, times = (jobs[row, i * TOGETHER + t] for row in range(3))
            q = far[n // 2, pl.ds(pl.multiple_of(n % 2 * R, R), R), :]
            taken.append((q, p, times.astype(f32)))
        tiles(taken, turned, scale, sums)
        return carry

    lax.fori_loop(0, (total + TOGETHER - 1) // TOGETHER, some, 0)


def far_kernel(seconds, place, *refs):
    far = refs[: len(seconds)]
    turned, scale, asked, sums_in, sums = refs[len(seconds) : len(seconds) + 5]
    jobs = refs[-1]
    sums[...] = sums_in[...]
    for rows, second in zip(far, seconds):
        add_far(rows, second, place, turned, scale, asked, sums, jobs)
    for theirs in refs[len(seconds) + 5 : -1]:
        theirs[...] = sums[2:]


def finish_kernel(rows, sums, received, out):
    for b in range(2):
        degree = sums[b, R : R + 1, :R] + received[b, R : R + 1, :R]
        column = jnp.broadcast_to(0.5 / degree, (R, R)).T
        for t in range(E // R):
            at = slice(t * R, (t + 1) * R)
            pulled = sums[b, :R, at] + received[b, :R, at]
            out[b, :, at] = 0.5 * rows[b, :, at] + pulled * column


def swaps(stage, swap):
    to = {1: (1, 0, 3, 2), 2: (3, 2, 1, 0), 3: (2, 3, 0, 1)}[swap]
    pairs = []
    for y in range(SIDE):
        for x in range(SIDE):
            for core in range(2):
                along_x = (core + stage) % 2 == 0
                to_x, to_y = (to[x], y) if along_x else (x, to[y])
                pairs.append(((y * SIDE + x) * 2 + core, (to_y * SIDE + to_x) * 2 + core))
    return pairs


def across_swaps(groups, devices):
    pairs = []
    for z in range(groups):
        for dev in range(devices):
            to = (z + 1 if (z + dev) % 2 == 0 else z - 1) % groups
            pairs.append((z * devices + dev, to * devices + dev))
    return pairs


def local(embeddings, neighbours):
    groups, devices = lax.axis_size("group"), lax.axis_size("dev")
    dev = lax.axis_index("dev").astype(jnp.int32)
    upper = (lax.axis_index("group").astype(jnp.int32) + dev) % 2 == 0
    place = jnp.where(jnp.arange(2) == 0, dev, upper.astype(jnp.int32))
    packed = pl.pallas_call(
        pack_kernel,
        out_shape=array((ROWS, E), bf16),
        in_specs=[pl.BlockSpec(memory_space=pltpu.HBM)] * 2,
        out_specs=whole(),
        scratch_shapes=[
            pltpu.SMEM(neighbours.shape, jnp.int32),
            pltpu.VMEM(embeddings.shape, f32),
            pltpu.SemaphoreType.DMA((5,)),
        ],
        cost_estimate=pl.CostEstimate(flops=1 << 18, bytes_accessed=3 << 18, transcendentals=0),
        compiler_params=pltpu.CompilerParams(vmem_limit_bytes=60 << 20),
    )(neighbours, embeddings)

    def along(value, stage, swap):
        return lax.ppermute(value, "dev", swaps(stage, swap))

    between = [(i, i ^ 1) for i in range(devices)]
    near = [along(packed, 0, swap) for swap in ORDER]
    other = lax.ppermute(packed, "dev", between)
    across = lax.ppermute(
        jnp.stack([packed, other]), ("group", "dev"), across_swaps(groups, devices)
    )
    near = jnp.stack([packed] + near)
    far = [along(near, 1, swap) for swap in ORDER]

    all_sums = array((4, R + 8, E), f32)
    turned, scale, asked, sums = call(
        local_kernel,
        (array((4, E, R), bf16), array((4, 8, R), f32), array((8, E), f32), all_sums),
        [whole()] * 2,
        200_000_000,
        2 << 20,
    )(packed, other)

    def add(rows, seconds, sums, last):
        def kernel(*refs):
            far_kernel(seconds, *refs)

        return call(
            kernel,
            (all_sums,) + (array((2, R + 8, E), f32),) * last,
            [scalars()] + [whole()] * (len(rows) + 4),
            200_000_000,
            2 << 20,
            [pltpu.SMEM((3, 8 * SIDE + TOGETHER), jnp.int32)],
        )(place, *rows, turned, scale, asked, sums)

    (sums,) = add([near], (0,), sums, 0)
    (sums,) = add(far[:1], ORDER[:1], sums, 0)
    sums = call(
        across_kernel, all_sums, [scalars()] + [whole()] * 6, 200_000_000, 2 << 20
    )(place, packed, other, across, turned, scale, sums)
    sums, theirs = add(far[1:], ORDER[1:], sums, 1)
    received = lax.ppermute(theirs, "dev", between)
    return call(
        finish_kernel,
        array(embeddings.shape, f32),
        [whole()] * 3,
        1 << 20,
        2 << 20,
    )(embeddings, sums, received)


def solution(mesh):
    in_specs = (P(("group", "dev"), None, None), P(("group", "dev"), None))
    out_specs = P(("group", "dev"), None, None)
    return jax.shard_map(local, mesh=mesh, in_specs=in_specs, out_specs=out_specs, check_vma=False)
```

```python
import jax
import jax.numpy as jnp
from jax import lax
from jax.experimental import pallas as pl
from jax.experimental.pallas import tpu as pltpu
from jax.sharding import PartitionSpec as P

KO = 4
KI = 3
R = 128
E = 512
SIDE = 4
ROWS = 2 * R + 8
TOGETHER = 4

inv_band = 40.0
eps = 1e-06

f32 = jnp.float32
bf16 = jnp.bfloat16


def whole():
    return pl.BlockSpec(memory_space=pltpu.VMEM)


def scalars():
    return pl.BlockSpec(memory_space=pltpu.SMEM)


def call(kernel, out_shape, in_specs, flops, nbytes, scratch=()):
    return pl.pallas_call(
        kernel,
        out_shape=out_shape,
        in_specs=in_specs,
        scratch_shapes=scratch,
        out_specs=jax.tree.map(lambda _: whole(), out_shape),
        cost_estimate=pl.CostEstimate(flops=flops, bytes_accessed=nbytes, transcendentals=0),
        compiler_params=pltpu.CompilerParams(vmem_limit_bytes=6 << 20),
    )


def array(shape, dtype):
    return jax.ShapeDtypeStruct(shape, dtype)


def column_scale(q):
    wide = q.astype(f32)
    return lax.rsqrt(jnp.sum(wide * wide, axis=1, keepdims=True) * (1.0 / E) + eps)


def tiles(jobs, turned, scale, sums):
    weighted = []
    for q, p, times in jobs:
        inner = jnp.dot(q, turned[p], preferred_element_type=f32)
        kernel = jnp.exp(inner * column_scale(q) * scale[p, 0:1, :])
        weighted.append(kernel * times)
    pulled = [
        lax.dot_general(
            w.astype(bf16), q, (((0,), (0,)), ((), ())), preferred_element_type=f32
        )
        for (q, p, times), w in zip(jobs, weighted)
    ]
    for (q, p, times), w, rows in zip(jobs, weighted, pulled):
        sums[p, R : R + 1, :R] += jnp.sum(w, axis=0, keepdims=True)
        sums[p, :R, :] += rows


def prepare(own, other, turned, scale, asked):
    lane = lax.broadcasted_iota(jnp.int32, (1, E), 1) // R
    for n, (rows, b) in enumerate(((own, 0), (own, 1), (other, 0), (other, 1))):
        block = rows[b * R : (b + 1) * R, :]
        turned[n] = block.T
        column = column_scale(block) * (inv_band / E)
        scale[n] = jnp.broadcast_to(column, (R, R)).T[:8]
    own_names = own[2 * R :, :].astype(f32)
    other_names = other[2 * R :, :].astype(f32)
    for j in range(KI):
        asked[j : j + 1, :] = jnp.where(
            lane < 2,
            jnp.where(lane == 0, own_names[j : j + 1], own_names[4 + j : 5 + j]),
            jnp.where(lane == 2, other_names[j : j + 1], other_names[4 + j : 5 + j]),
        )


def write_job(jobs, at, *job):
    for row, value in enumerate(job):
        jobs[row, at] = value


def across_jobs(piece, upper, own, other, across, jobs, total):
    for n, rows in enumerate((own, other)):
        near_names = rows[2 * R :, :].astype(f32)
        far_names = across[n, 2 * R :, :].astype(f32)
        for b in range(2):
            row = 4 * b + KI
            ours = jnp.max(near_names[row : row + 1, :R]).astype(jnp.int32)
            named = jnp.max(far_names[row : row + 1, :R]).astype(jnp.int32)
            far = jnp.clip(jnp.where(upper, ours, b), 0, 1)
            near = jnp.clip(jnp.where(upper, b, named), 0, 1)
            write_job(jobs, total, piece, 2 * n + far, 2 * n + near, 1)
            total = total + 1
    return total


def partner(at, swap):
    near = at + 1 - 2 * (at % 2)
    away = SIDE - 1 - at
    return jnp.where(swap == 0, at, jnp.where(swap == 1, near, jnp.where(swap == 2, away, (at + 2) % SIDE)))


def inner_jobs(pieces, place, asked, jobs, total):
    dev = place[0]
    y, x, core = dev // 8, dev // 2 % SIDE, dev % 2
    lane = lax.broadcasted_iota(jnp.int32, (1, E), 1) // R
    code = jnp.where(lane < 2, dev * 2 + lane, (dev + 1 - 2 * core) * 2 + lane - 2).astype(f32)
    digits = jnp.zeros((1, E), f32)
    places = []
    for piece, rows, firsts, second in pieces:
        for k, first in enumerate(firsts):
            from_x = partner(x, jnp.where(core == 0, first, second))
            from_y = partner(y, jnp.where(core == 0, second, first))
            source = (from_y * SIDE + from_x) * 2 + core
            names = rows[k, 2 * R :, :].astype(f32)
            for b in range(2):
                block = (source * 2 + b).astype(f32)
                count = jnp.zeros((1, E), f32)
                for j in range(KI):
                    count += jnp.where(names[4 * b + j : 4 * b + j + 1] == code, 1.0, 0.0)
                    count += jnp.where(asked[j : j + 1, :] == block, 1.0, 0.0)
                digits += count * float(4 ** len(places))
                places.append((piece, 2 * k + b))
    for p in range(4):
        word = jnp.max(digits[:, p * R : (p + 1) * R]).astype(jnp.int32)
        for n, (piece, block) in enumerate(places):
            times = (word >> (2 * n)) & 3
            write_job(jobs, total, piece, block, p, times)
            total = total + jnp.where(times > 0, 1, 0)
    return total


def run_jobs(far, turned, scale, sums, jobs, total, held):
    for n in range(TOGETHER - 1):
        write_job(jobs, total + n, 0, 0, 0, 0)

    def some(i, carry):
        taken = []
        for t in range(TOGETHER):
            piece, n, p, times = (jobs[row, i * TOGETHER + t] for row in range(4))
            for number, rows in enumerate(far):

                @pl.when(piece == number)
                def _():
                    held[t] = rows[n // 2, pl.ds(pl.multiple_of(n % 2 * R, R), R), :]

            taken.append((held[t], p, times.astype(f32)))
        tiles(taken, turned, scale, sums)
        return carry

    lax.fori_loop(0, (total + TOGETHER - 1) // TOGETHER, some, 0)


def first_kernel(origins, place, own, other, *refs):
    far = refs[: len(origins)]
    turned, scale, asked, sums, jobs, held = refs[len(origins) :]
    prepare(own, other, turned, scale, asked)
    sums[...] = jnp.zeros(sums.shape, f32)
    for b in range(2):
        write_job(jobs, b, 0, 1 - b, b, 2 * KO)
    total = jnp.int32(2)
    pieces = [(n, rows, *origins[n]) for n, rows in enumerate(far)]
    for n in range(0, len(pieces), 2):
        total = inner_jobs(pieces[n : n + 2], place, asked, jobs, total)
    run_jobs(far, turned, scale, sums, jobs, total, held)


def middle_kernel(origins, place, own, other, across, *refs):
    far = refs[: len(origins)]
    turned, scale, asked, sums_in, sums, jobs, held = refs[len(origins) :]
    sums[...] = sums_in[...]
    total = across_jobs(len(far), place[1] == 1, own, other, across, jobs, jnp.int32(0))
    pieces = [(n, rows, *origins[n]) for n, rows in enumerate(far)]
    for n in range(0, len(pieces), 2):
        total = inner_jobs(pieces[n : n + 2], place, asked, jobs, total)
    run_jobs((*far, across), turned, scale, sums, jobs, total, held)


def last_kernel(origins, place, *refs):
    far = refs[: len(origins)]
    turned, scale, asked, sums_in, mine, theirs, jobs, held, sums = refs[len(origins) :]
    sums[...] = sums_in[...]
    pieces = [(n, rows, *origins[n]) for n, rows in enumerate(far)]
    total = inner_jobs(pieces, place, asked, jobs, jnp.int32(0))
    run_jobs(far, turned, scale, sums, jobs, total, held)
    mine[...] = sums[:2]
    theirs[...] = sums[2:]


def finish_kernel(rows, sums, received, out):
    for b in range(2):
        degree = sums[b, R : R + 1, :R] + received[b, R : R + 1, :R]
        column = jnp.broadcast_to(0.5 / degree, (R, R)).T
        for t in range(E // R):
            at = slice(t * R, (t + 1) * R)
            pulled = sums[b, :R, at] + received[b, :R, at]
            out[b, :, at] = 0.5 * rows[b, :, at] + pulled * column


def swaps(stage, swap):
    to = {1: (1, 0, 3, 2), 2: (3, 2, 1, 0), 3: (2, 3, 0, 1)}[swap]
    pairs = []
    for y in range(SIDE):
        for x in range(SIDE):
            for core in range(2):
                along_x = (core + stage) % 2 == 0
                to_x, to_y = (to[x], y) if along_x else (x, to[y])
                pairs.append(((y * SIDE + x) * 2 + core, (to_y * SIDE + to_x) * 2 + core))
    return pairs


def across_swaps(groups, devices):
    pairs = []
    for z in range(groups):
        for dev in range(devices):
            to = (z + 1 if (z + dev) % 2 == 0 else z - 1) % groups
            pairs.append((z * devices + dev, to * devices + dev))
    return pairs


def local(embeddings, neighbours):
    groups, devices = lax.axis_size("group"), lax.axis_size("dev")
    dev = lax.axis_index("dev").astype(jnp.int32)
    upper = (lax.axis_index("group").astype(jnp.int32) + dev) % 2 == 0
    place = jnp.where(jnp.arange(2) == 0, dev, upper.astype(jnp.int32))
    names = neighbours[:, KO:]
    names = jnp.where(jnp.arange(KI + 1) < KI, names % (2 * devices), names % 2).astype(bf16)
    packed = jnp.concatenate(
        [
            embeddings.astype(bf16).reshape(2 * R, E),
            jnp.broadcast_to(names.reshape(8, 1), (8, E)),
        ]
    )

    def along(value, stage, swap):
        return lax.ppermute(value, "dev", swaps(stage, swap))

    between = [(i, i ^ 1) for i in range(devices)]
    opposite = along(packed, 0, 3)
    one = along(packed, 0, 1)
    two = along(packed, 0, 2)
    other = lax.ppermute(packed, "dev", between)
    even = jnp.stack([packed, opposite])
    even_two = along(even, 1, 2)
    odd = jnp.stack([one, two])
    odd_one = along(odd, 1, 1)
    even_one = along(even, 1, 1)
    odd_two = along(odd, 1, 2)
    across = lax.ppermute(
        jnp.stack([packed, other]), ("group", "dev"), across_swaps(groups, devices)
    )
    even_far = along(even_two, 1, 1)
    odd_far = along(odd_one, 1, 2)

    all_sums, two_sums = array((4, R + 8, E), f32), array((2, R + 8, E), f32)

    def run(kernel, origins, out_shape, *args, scratch=()):
        def body(*refs):
            kernel(origins, *refs)

        return call(
            body,
            out_shape,
            [scalars()] + [whole()] * len(args),
            200_000_000,
            2 << 20,
            [
                pltpu.SMEM((4, 16 * len(origins) + 8 + TOGETHER), jnp.int32),
                pltpu.VMEM((TOGETHER, R, E), bf16),
                *scratch,
            ],
        )(place, *args)

    own_far, both = (0, 3), (1, 2)
    turned, scale, asked, sums = run(
        first_kernel,
        ((own_far, 0), (both, 0), (own_far, 2), (both, 1)),
        (array((4, E, R), bf16), array((4, 8, R), f32), array((8, E), f32), all_sums),
        packed, other, even, odd, even_two, odd_one,
    )
    sums = run(
        middle_kernel,
        ((own_far, 1), (both, 2)),
        all_sums,
        packed, other, across, even_one, odd_two, turned, scale, asked, sums,
    )
    sums, theirs = run(
        last_kernel,
        ((own_far, 3), (both, 3)),
        (two_sums, two_sums),
        even_far, odd_far, turned, scale, asked, sums,
        scratch=[pltpu.VMEM(all_sums.shape, f32)],
    )
    received = lax.ppermute(theirs, "dev", between)
    return call(
        finish_kernel,
        array(embeddings.shape, f32),
        [whole()] * 3,
        1 << 20,
        2 << 20,
    )(embeddings, sums, received)


def solution(mesh):
    in_specs = (P(("group", "dev"), None, None), P(("group", "dev"), None))
    out_specs = P(("group", "dev"), None, None)
    return jax.shard_map(local, mesh=mesh, in_specs=in_specs, out_specs=out_specs, check_vma=False)
```

```python
import jax
import jax.numpy as jnp
from jax import lax
from jax.experimental import pallas as pl
from jax.experimental.pallas import tpu as pltpu
from jax.sharding import PartitionSpec as P

KO = 4
KI = 3
R = 128
E = 512
SIDE = 4
ROWS = 2 * R + 8
TOGETHER = 4

inv_band = 40.0
eps = 1e-06

f32 = jnp.float32
bf16 = jnp.bfloat16


def whole():
    return pl.BlockSpec(memory_space=pltpu.VMEM)


def scalars():
    return pl.BlockSpec(memory_space=pltpu.SMEM)


def call(kernel, out_shape, in_specs, flops, nbytes, scratch=()):
    return pl.pallas_call(
        kernel,
        out_shape=out_shape,
        in_specs=in_specs,
        scratch_shapes=scratch,
        out_specs=jax.tree.map(lambda _: whole(), out_shape),
        cost_estimate=pl.CostEstimate(flops=flops, bytes_accessed=nbytes, transcendentals=0),
        compiler_params=pltpu.CompilerParams(vmem_limit_bytes=6 << 20),
    )


def array(shape, dtype):
    return jax.ShapeDtypeStruct(shape, dtype)


def column_scale(q):
    wide = q.astype(f32)
    return lax.rsqrt(jnp.sum(wide * wide, axis=1, keepdims=True) * (1.0 / E) + eps)


def tiles(jobs, turned, scale, sums):
    weighted = []
    for q, p, times in jobs:
        inner = jnp.dot(q, turned[p], preferred_element_type=f32)
        kernel = jnp.exp(inner * column_scale(q) * scale[p, 0:1, :])
        weighted.append(kernel * times)
    pulled = [
        lax.dot_general(
            w.astype(bf16), q, (((0,), (0,)), ((), ())), preferred_element_type=f32
        )
        for (q, p, times), w in zip(jobs, weighted)
    ]
    for (q, p, times), w, rows in zip(jobs, weighted, pulled):
        sums[p, R : R + 1, :R] += jnp.sum(w, axis=0, keepdims=True)
        sums[p, :R, :] += rows


def prepare(own, other, turned, scale, asked):
    lane = lax.broadcasted_iota(jnp.int32, (1, E), 1) // R
    for n, (rows, b) in enumerate(((own, 0), (own, 1), (other, 0), (other, 1))):
        block = rows[b * R : (b + 1) * R, :]
        turned[n] = block.T
        column = column_scale(block) * (inv_band / E)
        scale[n] = jnp.broadcast_to(column, (R, R)).T[:8]
    own_names = own[2 * R :, :].astype(f32)
    other_names = other[2 * R :, :].astype(f32)
    for j in range(KI):
        asked[j : j + 1, :] = jnp.where(
            lane < 2,
            jnp.where(lane == 0, own_names[j : j + 1], own_names[4 + j : 5 + j]),
            jnp.where(lane == 2, other_names[j : j + 1], other_names[4 + j : 5 + j]),
        )


def write_job(jobs, at, *job):
    for row, value in enumerate(job):
        jobs[row, at] = value


def across_jobs(piece, upper, own, other, across, jobs, total):
    for n, rows in enumerate((own, other)):
        near_names = rows[2 * R :, :].astype(f32)
        far_names = across[n, 2 * R :, :].astype(f32)
        for b in range(2):
            row = 4 * b + KI
            ours = jnp.max(near_names[row : row + 1, :R]).astype(jnp.int32)
            named = jnp.max(far_names[row : row + 1, :R]).astype(jnp.int32)
            far = jnp.clip(jnp.where(upper, ours, b), 0, 1)
            near = jnp.clip(jnp.where(upper, b, named), 0, 1)
            write_job(jobs, total, piece, 2 * n + far, 2 * n + near, 1)
            total = total + 1
    return total


def partner(at, swap):
    near = at + 1 - 2 * (at % 2)
    away = SIDE - 1 - at
    return jnp.where(swap == 0, at, jnp.where(swap == 1, near, jnp.where(swap == 2, away, (at + 2) % SIDE)))


def inner_jobs(pieces, place, asked, jobs, total):
    dev = place[0]
    y, x, core = dev // 8, dev // 2 % SIDE, dev % 2
    lane = lax.broadcasted_iota(jnp.int32, (1, E), 1) // R
    code = jnp.where(lane < 2, dev * 2 + lane, (dev + 1 - 2 * core) * 2 + lane - 2).astype(f32)
    digits = jnp.zeros((1, E), f32)
    places = []
    for piece, rows, firsts, second in pieces:
        for k, first in enumerate(firsts):
            from_x = partner(x, jnp.where(core == 0, first, second))
            from_y = partner(y, jnp.where(core == 0, second, first))
            source = (from_y * SIDE + from_x) * 2 + core
            names = rows[k, 2 * R :, :].astype(f32)
            for b in range(2):
                block = (source * 2 + b).astype(f32)
                count = jnp.zeros((1, E), f32)
                for j in range(KI):
                    count += jnp.where(names[4 * b + j : 4 * b + j + 1] == code, 1.0, 0.0)
                    count += jnp.where(asked[j : j + 1, :] == block, 1.0, 0.0)
                digits += count * float(4 ** len(places))
                places.append((piece, 2 * k + b))
    for p in range(4):
        word = jnp.max(digits[:, p * R : (p + 1) * R]).astype(jnp.int32)
        for n, (piece, block) in enumerate(places):
            times = (word >> (2 * n)) & 3
            write_job(jobs, total, piece, block, p, times)
            total = total + jnp.where(times > 0, 1, 0)
    return total


def run_jobs(far, turned, scale, sums, jobs, total, held):
    for n in range(TOGETHER - 1):
        write_job(jobs, total + n, 0, 0, 0, 0)

    def some(i, carry):
        taken = []
        for t in range(TOGETHER):
            piece, n, p, times = (jobs[row, i * TOGETHER + t] for row in range(4))
            for number, rows in enumerate(far):

                @pl.when(piece == number)
                def _():
                    held[t] = rows[n // 2, pl.ds(pl.multiple_of(n % 2 * R, R), R), :]

            taken.append((held[t], p, times.astype(f32)))
        tiles(taken, turned, scale, sums)
        return carry

    lax.fori_loop(0, (total + TOGETHER - 1) // TOGETHER, some, 0)


def first_kernel(origins, place, own, other, *refs):
    far = refs[: len(origins)]
    turned, scale, asked, sums, jobs, held = refs[len(origins) :]
    prepare(own, other, turned, scale, asked)
    sums[...] = jnp.zeros(sums.shape, f32)
    for b in range(2):
        write_job(jobs, b, 0, 1 - b, b, 2 * KO)
    total = jnp.int32(2)
    pieces = [(n, rows, *origins[n]) for n, rows in enumerate(far)]
    for n in range(0, len(pieces), 2):
        total = inner_jobs(pieces[n : n + 2], place, asked, jobs, total)
    run_jobs(far, turned, scale, sums, jobs, total, held)


def middle_kernel(origins, place, own, other, across, *refs):
    far = refs[: len(origins)]
    turned, scale, asked, sums_in, sums, jobs, held = refs[len(origins) :]
    sums[...] = sums_in[...]
    total = across_jobs(len(far), place[1] == 1, own, other, across, jobs, jnp.int32(0))
    pieces = [(n, rows, *origins[n]) for n, rows in enumerate(far)]
    for n in range(0, len(pieces), 2):
        total = inner_jobs(pieces[n : n + 2], place, asked, jobs, total)
    run_jobs((*far, across), turned, scale, sums, jobs, total, held)


def last_kernel(origins, place, *refs):
    far = refs[: len(origins)]
    turned, scale, asked, sums_in, mine, theirs, jobs, held, sums = refs[len(origins) :]
    sums[...] = sums_in[...]
    pieces = [(n, rows, *origins[n]) for n, rows in enumerate(far)]
    total = inner_jobs(pieces, place, asked, jobs, jnp.int32(0))
    run_jobs(far, turned, scale, sums, jobs, total, held)
    mine[...] = sums[:2]
    theirs[...] = sums[2:]


def finish_kernel(rows, sums, received, out):
    for b in range(2):
        degree = sums[b, R : R + 1, :R] + received[b, R : R + 1, :R]
        column = jnp.broadcast_to(0.5 / degree, (R, R)).T
        for t in range(E // R):
            at = slice(t * R, (t + 1) * R)
            pulled = sums[b, :R, at] + received[b, :R, at]
            out[b, :, at] = 0.5 * rows[b, :, at] + pulled * column


def swaps(stage, swap):
    to = {1: (1, 0, 3, 2), 2: (3, 2, 1, 0), 3: (2, 3, 0, 1)}[swap]
    pairs = []
    for y in range(SIDE):
        for x in range(SIDE):
            for core in range(2):
                along_x = (core + stage) % 2 == 0
                to_x, to_y = (to[x], y) if along_x else (x, to[y])
                pairs.append(((y * SIDE + x) * 2 + core, (to_y * SIDE + to_x) * 2 + core))
    return pairs


def across_swaps(groups, devices):
    pairs = []
    for z in range(groups):
        for dev in range(devices):
            to = (z + 1 if (z + dev) % 2 == 0 else z - 1) % groups
            pairs.append((z * devices + dev, to * devices + dev))
    return pairs


def local(embeddings, neighbours):
    groups, devices = lax.axis_size("group"), lax.axis_size("dev")
    dev = lax.axis_index("dev").astype(jnp.int32)
    upper = (lax.axis_index("group").astype(jnp.int32) + dev) % 2 == 0
    place = jnp.where(jnp.arange(2) == 0, dev, upper.astype(jnp.int32))
    names = neighbours[:, KO:]
    names = jnp.where(jnp.arange(KI + 1) < KI, names % (2 * devices), names % 2).astype(bf16)
    packed = jnp.concatenate(
        [
            embeddings.astype(bf16).reshape(2 * R, E),
            jnp.broadcast_to(names.reshape(8, 1), (8, E)),
        ]
    )

    def along(value, stage, swap):
        return lax.ppermute(value, "dev", swaps(stage, swap))

    between = [(i, i ^ 1) for i in range(devices)]
    opposite = along(packed, 0, 3)
    one = along(packed, 0, 1)
    two = along(packed, 0, 2)
    other = lax.ppermute(packed, "dev", between)
    even = jnp.stack([packed, opposite])
    even_two = along(even, 1, 2)
    odd = jnp.stack([one, two])
    odd_one = along(odd, 1, 1)
    even_one = along(even, 1, 1)
    odd_two = along(odd, 1, 2)
    across = lax.ppermute(
        jnp.concatenate([packed, other]), ("group", "dev"), across_swaps(groups, devices)
    ).reshape(2, ROWS, E)
    even_far = along(even_two, 1, 1)
    odd_far = along(odd_one, 1, 2)

    all_sums, two_sums = array((4, R + 8, E), f32), array((2, R + 8, E), f32)

    def run(kernel, origins, out_shape, *args, scratch=()):
        def body(*refs):
            kernel(origins, *refs)

        return call(
            body,
            out_shape,
            [scalars()] + [whole()] * len(args),
            200_000_000,
            2 << 20,
            [
                pltpu.SMEM((4, 16 * len(origins) + 8 + TOGETHER), jnp.int32),
                pltpu.VMEM((TOGETHER, R, E), bf16),
                *scratch,
            ],
        )(place, *args)

    own_far, both = (0, 3), (1, 2)
    turned, scale, asked, sums = run(
        first_kernel,
        ((own_far, 0), (both, 0), (own_far, 2), (both, 1)),
        (array((4, E, R), bf16), array((4, 8, R), f32), array((8, E), f32), all_sums),
        packed, other, even, odd, even_two, odd_one,
    )
    sums = run(
        middle_kernel,
        ((own_far, 1), (both, 2)),
        all_sums,
        packed, other, across, even_one, odd_two, turned, scale, asked, sums,
    )
    sums, theirs = run(
        last_kernel,
        ((own_far, 3), (both, 3)),
        (two_sums, two_sums),
        even_far, odd_far, turned, scale, asked, sums,
        scratch=[pltpu.VMEM(all_sums.shape, f32)],
    )
    received = lax.ppermute(theirs, "dev", between)
    return call(
        finish_kernel,
        array(embeddings.shape, f32),
        [whole()] * 3,
        1 << 20,
        2 << 20,
    )(embeddings, sums, received)


def solution(mesh):
    in_specs = (P(("group", "dev"), None, None), P(("group", "dev"), None))
    out_specs = P(("group", "dev"), None, None)
    return jax.shard_map(local, mesh=mesh, in_specs=in_specs, out_specs=out_specs, check_vma=False)
```
